128 devices in a mesh: grp: 8 (over x, core), sub: 16 (over z, y).
Axes of the slice: x: 4, y: 4, z: 4, core: 2. Of those that a mesh axis runs over, the one named last changes fastest.
Arguments:
- points: bfloat16 [131072, 1024], P(('grp', 'sub')), may hold values from -16 to 16
- level1_ids: int32 [131072], P(('grp', 'sub')), may hold values from 0 to 1023
- level2_ids: int32 [131072], P(('grp', 'sub')), may hold values from 0 to 8191, as said below
- level3_ids: int32 [131072], P(('grp', 'sub')), may hold values from 0 to 255
- needed: int32 [128, 128], P(('grp', 'sub')), may hold values from 0 to 32767, as said below
- centroids1: bfloat16 [262144, 1024], P(('grp', 'sub')), may hold values from -6 to 6
- centroids2: bfloat16 [8, 8192, 1024], P('grp', 'sub'), may hold values from -3 to 3
- centroids3: bfloat16 [256, 1024], replicated, may hold values from -6 to 6
Outputs:
- level1_new: float32 [262144, 1024], P(('grp', 'sub'))
- level2_new: float32 [8, 8192, 1024], P('grp', 'sub')
- level3_new: float32 [256, 1024], replicated
The draws below stay inside these ranges and needn't reach their ends.
Inputs may be any that keep to these rules, and one draw needn't show every extreme that they name: `needed`: each row lists distinct blocks; a row names at most 2 blocks held by one device (blocks of device o are o * 256 to o * 256 + 255), and names exactly 2 of some device's blocks. `level2_ids`: of one device's points, at most 128 have level-2 ids in any one range r * 8192 // 16 to (r + 1) * 8192 // 16 - 1, and exactly 128 in some range.
All inputs are finite; a program needn't handle non-finite values.
Results may differ from the reference program's by a relative error of at most 0.0055.
Values may be sent and summed in bfloat16 or wider, within the bound.
No kernel may reach another device: no remote copies, remote signals or barrier semaphores. Data moves between devices by JAX's collectives and lax.ppermute only.
A program may use at most 128 MiB of HBM per device.

```python
import math
import jax
import jax.numpy as jnp
from jax import lax

D = 1024
BLK = 8
CAP = 2
K2 = 8192
K3 = 256
PTS_DEV = 1024
K1 = 262144
NB_DEV = 256
NEED = 128
CAP2 = 128
POINTS = 131072
N_GRP = 8
N_SUB = 16
DEVICES = 128


def level3_labels(key):
    base = jax.random.fold_in(key, 31)

    def per_device(dev_key, device):
        first_key, second_key, third_key = jax.random.split(dev_key, 3)
        home_cluster = device * K3 // DEVICES
        width_near = max(K3 // DEVICES, 1)
        near_ids = home_cluster + jax.random.randint(first_key, (PTS_DEV,), 0, width_near)
        far_ids = jax.random.randint(second_key, (PTS_DEV,), 0, K3)
        choose_near = jax.random.randint(third_key, (PTS_DEV,), 0, 4) < 3
        return jnp.where(choose_near, near_ids, far_ids)
    keys = jax.random.split(base, DEVICES)
    return jax.vmap(per_device)(keys, jnp.arange(DEVICES)).reshape(-1).astype(jnp.int32)


def needed_lists(key):
    base = jax.random.fold_in(key, 61)

    def per_device(dev_key):
        first_key, second_key, third_key = jax.random.split(dev_key, 3)
        hot_owner = jax.random.randint(first_key, (), 0, DEVICES)
        slot_ids = jnp.arange(DEVICES * CAP)
        random_bits = jax.random.randint(second_key, (DEVICES * CAP,), 0, 1 << 18)
        scores = random_bits * (DEVICES * CAP) + slot_ids + jnp.where(slot_ids // CAP == hot_owner, 1 << 30, 0)
        chosen = lax.top_k(scores, NEED)[1]
        owner_of = chosen // CAP
        offset = jax.random.randint(third_key, (DEVICES,), 0, NB_DEV)
        local_block = (offset[owner_of] + chosen % CAP) % NB_DEV
        return owner_of * NB_DEV + local_block
    return jax.vmap(per_device)(jax.random.split(base, DEVICES)).astype(jnp.int32)


def draw_needed(key, part):
    return needed_lists(key)


def draw_level1_ids(key, part):
    first_key, second_key = jax.random.split(jax.random.fold_in(key, 71))
    picks = jax.random.randint(first_key, (DEVICES, PTS_DEV), 0, NEED)
    within = jax.random.randint(second_key, (DEVICES, PTS_DEV), 0, BLK)
    return (picks * BLK + within).reshape(-1).astype(jnp.int32)


def draw_level2_ids(key, part):
    base = jax.random.fold_in(key, 51)
    group_keys = jax.random.split(jax.random.fold_in(base, 1), DEVICES // N_SUB)
    hot_by_group = jax.vmap(lambda group_key: jax.random.randint(group_key, (), 0, N_SUB))(group_keys)
    shard_rows = K2 // N_SUB

    def per_device(dev_key, hot_owner):
        first_key, second_key, third_key = jax.random.split(dev_key, 3)
        slot_ids = jnp.arange(N_SUB * CAP2)
        slot_owner = slot_ids // CAP2
        random_bits = jax.random.randint(first_key, (N_SUB * CAP2,), 0, 1 << 16)
        scores = random_bits * (N_SUB * CAP2) + slot_ids + jnp.where(slot_owner == hot_owner, 1 << 30, 0)
        chosen = lax.top_k(scores, PTS_DEV)[1]
        chosen = chosen[jax.random.permutation(second_key, PTS_DEV)]
        local_block = jax.random.randint(third_key, (PTS_DEV,), 0, shard_rows)
        return chosen // CAP2 * shard_rows + local_block
    keys = jax.random.split(base, DEVICES)
    hot_each = jnp.repeat(hot_by_group, N_SUB)
    return jax.vmap(per_device)(keys, hot_each).reshape(-1).astype(jnp.int32)


def draw_level3_ids(key, part):
    return level3_labels(key)


def draw_points(key, part):
    labels = level3_labels(key)
    base = jax.random.fold_in(key, 41)
    first_key, second_key, third_key = jax.random.split(base, 3)
    offset_key = jax.random.fold_in(base, 5)
    cluster_means = jnp.clip(jax.random.normal(first_key, (K3, D), jnp.float32), -4.0, 4.0)
    device_shift = jnp.clip(jax.random.normal(offset_key, (DEVICES, D), jnp.float32), -2.0, 2.0)
    device_of = jnp.arange(PTS_DEV * DEVICES) // PTS_DEV
    row_scale = jnp.exp(jax.random.uniform(second_key, (PTS_DEV * DEVICES, 1), jnp.float32, math.log(0.3), math.log(3.0)))
    jitter = jnp.clip(jax.random.normal(third_key, (PTS_DEV * DEVICES, D), jnp.float32), -4.0, 4.0)
    values = cluster_means[labels] + device_shift[device_of] + row_scale * jitter
    return jnp.clip(values, -16.0, 16.0).astype(jnp.bfloat16)


def shard_levels(stream_key, dims, pieces, low, largest):
    def one(position, blocks):
        steps = jax.random.uniform(jax.random.fold_in(jax.random.fold_in(stream_key, 6), position), (blocks,), jnp.float32, low / len(pieces), largest / len(pieces))
        return jnp.repeat(jnp.exp(steps), dims[position] // blocks).reshape((-1,) + (1,) * (len(dims) - position - 1))

    level = one(*pieces[0])
    for cut in pieces[1:]:
        level = level * one(*cut)
    return level


def centred(rng, extent, deviation, bound, shards=(), kind=jnp.bfloat16):
    array = deviation * jax.random.normal(rng, extent, jnp.float32)
    if shards:
        array = array * shard_levels(rng, extent, shards, -0.22, 0.18)
    return jnp.clip(array, -bound, bound).astype(kind)


def setup_inputs(seed: int = 0) -> dict:
    seeds = jax.random.split(jax.random.key(seed), 9)
    return {
        "points": draw_points(jax.random.fold_in(seeds[8], 71), 0),
        "level1_ids": draw_level1_ids(jax.random.fold_in(seeds[8], 71), 0),
        "level2_ids": draw_level2_ids(jax.random.fold_in(seeds[8], 71), 0),
        "level3_ids": draw_level3_ids(jax.random.fold_in(seeds[8], 71), 0),
        "needed": draw_needed(jax.random.fold_in(seeds[8], 71), 0),
        "centroids1": centred(seeds[5], (K1, D), 1.0, 6.0, ((0, 128),)),
        "centroids2": centred(seeds[6], (N_GRP, K2, D), 0.5, 3.0, ((0, 8), (1, 16))),
        "centroids3": centred(seeds[7], (K3, D), 1.0, 6.0),
    }


def rounded(values):
    return lax.optimization_barrier(values.astype(jnp.bfloat16)).astype(jnp.float32)


def reference(points, level1_ids, level2_ids, level3_ids, needed, centroids1, centroids2, centroids3):
    device_of = (jnp.arange(POINTS, dtype=jnp.int32) // PTS_DEV).astype(jnp.int32)
    entry = (level1_ids // BLK).astype(jnp.int32)
    global1 = (needed[device_of, entry] * BLK + level1_ids % BLK).astype(jnp.int32)
    values = points.astype(jnp.float32)
    nearest = centroids1[global1].astype(jnp.float32)
    spread = jnp.sum((values - nearest) ** 2, axis=1) / D
    weight = rounded(1.0 / (1.0 + spread))
    weighted = weight[:, None] * values
    sums1 = jax.ops.segment_sum(weighted, global1, num_segments=K1)
    mass1 = jax.ops.segment_sum(weight, global1, num_segments=K1)
    level1_new = (centroids1.astype(jnp.float32) + sums1) / (1.0 + mass1[:, None])

    group_index = jnp.arange(DEVICES, dtype=jnp.int32) // N_SUB

    def add_device(totals, inputs):
        sums_acc, mass_acc = totals
        row_block, labels, masses, group_at = inputs
        device_sums = rounded(jax.ops.segment_sum(row_block, labels, num_segments=K2))
        device_mass = rounded(jax.ops.segment_sum(masses, labels, num_segments=K2))
        return (sums_acc.at[group_at].add(device_sums), mass_acc.at[group_at].add(device_mass)), None

    start = (jnp.zeros((N_GRP, K2, D), jnp.float32), jnp.zeros((N_GRP, K2), jnp.float32))
    (sums2, mass2), _ = lax.scan(add_device, start, (weighted.reshape(DEVICES, PTS_DEV, D), level2_ids.reshape(DEVICES, PTS_DEV), weight.reshape(DEVICES, PTS_DEV), group_index))
    level2_new = (centroids2.astype(jnp.float32) + sums2) / (1.0 + mass2[:, :, None])

    sums3 = jax.ops.segment_sum(weighted, level3_ids, num_segments=K3)
    mass3 = jax.ops.segment_sum(weight, level3_ids, num_segments=K3)
    level3_new = (centroids3.astype(jnp.float32) + sums3) / (1.0 + mass3[:, None])
    return level1_new, level2_new, level3_new
```

```python
import jax
import jax.numpy as jnp
from jax import lax
from jax.experimental import pallas as pl
from jax.experimental.pallas import tpu as pltpu
from jax.sharding import PartitionSpec as P

D = 1024
K1_DEV = 2048
BLK = 8
CAP = 2
K2 = 8192
K3 = 256
CAP2 = 128
TILE = 256
BF = jnp.bfloat16
F32 = jnp.float32
I32 = jnp.int32


def full(shape):
    return pl.BlockSpec(shape, lambda *_: (0,) * len(shape))


ANY = pl.BlockSpec(memory_space=pl.ANY)


def iota(shape, axis):
    return lax.broadcasted_iota(I32, shape, axis)


def route_kernel(ids_ref, pts_ref, out_ref, rank_ref, local_ref, slot_scr):
    step = pl.program_id(0)
    n = pts_ref.shape[0]
    subs = local_ref.shape[0]
    rows = K2 // subs
    chunk = out_ref.shape[0]

    @pl.when(step == 0)
    def _():
        ids = ids_ref[...]
        owner = ids // rows
        local = ids - owner * rows
        hot = (jnp.broadcast_to(owner, (subs, n)) == iota((subs, n), 0)).astype(F32)
        upper = (iota((n, n), 0) < iota((n, n), 1)).astype(F32).astype(BF)
        before = jnp.dot(hot.astype(BF), upper, preferred_element_type=F32)
        rank = jnp.sum(before * hot, axis=0, keepdims=True)
        slot_scr[...] = owner * CAP2 + rank.astype(I32)
        rank_col = jnp.transpose(jnp.broadcast_to(rank, (128, n)))
        rank_ref[...] = rank_col.astype(I32)
        hot_rank = (rank_col.astype(I32) == iota((n, CAP2), 1)).astype(F32).astype(BF)
        high = local // 256
        low = local - high * 256
        low_hot = (hot * low.astype(F32)).astype(BF)
        high_hot = (hot * high.astype(F32)).astype(BF)
        local_ref[...] = jnp.dot(low_hot, hot_rank, preferred_element_type=F32) + 256.0 * jnp.dot(
            high_hot, hot_rank, preferred_element_type=F32
        )

    slots = jnp.broadcast_to(slot_scr[...], (chunk, n))
    perm = (slots == iota((chunk, n), 0) + step * chunk).astype(F32).astype(BF)
    out_ref[...] = jnp.dot(perm, pts_ref[...], preferred_element_type=F32).astype(BF)


def route(ids2, points, subs):
    n = points.shape[0]
    total = subs * CAP2
    chunk = 512
    return pl.pallas_call(
        route_kernel,
        grid=(total // chunk,),
        in_specs=[full((1, n)), full((n, D))],
        out_specs=[
            pl.BlockSpec((chunk, D), lambda i: (i, 0)),
            full((n, 128)),
            full((subs, CAP2)),
        ],
        out_shape=[
            jax.ShapeDtypeStruct((total, D), BF),
            jax.ShapeDtypeStruct((n, 128), I32),
            jax.ShapeDtypeStruct((subs, CAP2), F32),
        ],
        scratch_shapes=[pltpu.VMEM((1, n), I32)],
        name="route",
    )(ids2.reshape(1, n), points)


def serve_kernel(asked, table_ref, out_ref, sem):
    count = out_ref.shape[0]

    def one(i, carry):
        pltpu.make_async_copy(table_ref.at[jnp.maximum(asked[i], 0)], out_ref.at[i], sem).start()
        return carry

    lax.fori_loop(0, count, one, 0, unroll=8)
    pltpu.make_async_copy(out_ref, out_ref, sem).wait()


def serve(asked, table):
    return pl.pallas_call(
        serve_kernel,
        grid_spec=pltpu.PrefetchScalarGridSpec(
            num_scalar_prefetch=1,
            grid=(),
            in_specs=[pl.BlockSpec(memory_space=pltpu.VMEM)],
            out_specs=ANY,
            scratch_shapes=[pltpu.SemaphoreType.DMA],
        ),
        out_shape=jax.ShapeDtypeStruct((asked.shape[0], BLK, D), BF),
        name="serve",
    )(asked, table)


def weigh_kernel(
    slot, fetched_ref, col1_ref, row1_ref, row2_ref, row3_ref, rank_ref, local_ref, pts_ref,
    sums_ref, small_ref, meta_ref,
    near_scr, sum_scr, w_scr, ext_scr, sem_in, sem_out,
):
    n = pts_ref.shape[0]
    need = near_scr.shape[0]
    rows = need * BLK

    def fetch(e, carry):
        pltpu.make_async_copy(fetched_ref.at[slot[e]], near_scr.at[e], sem_in).start()
        return carry

    lax.fori_loop(0, need, fetch, 0, unroll=8)
    ext_scr[...] = jnp.zeros(ext_scr.shape, F32)
    pltpu.make_async_copy(near_scr, near_scr, sem_in).wait()
    near = near_scr[...].reshape(rows, D)
    step = 256
    for c in range(n // step):
        col = col1_ref[c * step : (c + 1) * step, :]
        hot = jnp.concatenate(
            [(col == iota((step, 128), 1) + 128 * t).astype(F32) for t in range(rows // 128)], axis=1
        ).astype(BF)
        nearest = jnp.dot(hot, near, preferred_element_type=F32)
        diff = pts_ref[c * step : (c + 1) * step, :].astype(F32) - nearest
        spread = jnp.sum(diff * diff, axis=1, keepdims=True) / D
        w = (1.0 / (1.0 + spread)).astype(BF).astype(F32)
        w_scr[c * step : (c + 1) * step, :] = jnp.broadcast_to(w, (step, 128))
    w_col = w_scr[...]
    w_row = jnp.transpose(w_col)[0:1, :]

    def weighted(row_ids, count, first):
        same = jnp.broadcast_to(row_ids, (count, n)) == iota((count, n), 0) + first
        return jnp.where(same, jnp.broadcast_to(w_row, (count, n)), 0.0)

    lane = iota((BLK, 128), 1)
    tile = iota((K3, 128), 1)

    hot3 = weighted(row3_ref[...], K3, 0)
    sums3 = jnp.dot(hot3.astype(BF), pts_ref[...], preferred_element_type=F32).astype(BF)
    mass3 = jnp.broadcast_to(jnp.sum(hot3, axis=1, keepdims=True), (K3, 128))
    high3 = mass3.astype(BF).astype(F32)
    ext3 = jnp.where(tile == 4, high3, 0.0) + jnp.where(tile == 5, mass3 - high3, 0.0)
    wide = D // TILE
    devices = small_ref.shape[0]
    for o in range(devices):
        b, c = o // wide, o % wide
        small_ref[o, :, 0:TILE] = sums3[BLK * b : BLK * (b + 1), TILE * c : TILE * (c + 1)]

    part = 256
    for c in range(rows // part):
        hot1 = weighted(row1_ref[...], part, c * part)
        sums1 = jnp.dot(hot1.astype(BF), pts_ref[...], preferred_element_type=F32).astype(BF)
        sum_scr[c * (part // BLK) : (c + 1) * (part // BLK)] = sums1.reshape(part // BLK, BLK, D)
        mass1 = jnp.broadcast_to(jnp.sum(hot1, axis=1, keepdims=True), (part, 128))
        for k in range(part // BLK):
            e = c * (part // BLK) + k
            s = slot[e]
            pltpu.make_async_copy(sum_scr.at[e], sums_ref.at[s], sem_out).start()
            m = mass1[k * BLK : (k + 1) * BLK, :]
            high = m.astype(BF).astype(F32)
            o = s // CAP
            at = (s - o * CAP) * 2
            ext_scr[o] = ext_scr[o] + jnp.where(lane == at, high, 0.0) + jnp.where(
                lane == at + 1, m - high, 0.0
            )
    for o in range(devices):
        b = o // wide
        small_ref[o, :, TILE:] = (ext_scr[o] + ext3[BLK * b : BLK * (b + 1), :]).astype(BF)

    subs = meta_ref.shape[0]
    owner = row2_ref[...] // (K2 // subs)
    hot_owner = (jnp.broadcast_to(owner, (subs, n)) == iota((subs, n), 0)).astype(F32).astype(BF)
    hot_rank = jnp.where(rank_ref[...] == iota((n, CAP2), 1), w_col, 0.0).astype(BF)
    w_slots = jnp.dot(hot_owner, hot_rank, preferred_element_type=F32)
    meta_ref[...] = jnp.zeros(meta_ref.shape, F32)
    for t in range(subs):
        meta_ref[t, 0:1, :] = w_slots[t : t + 1, :]
        meta_ref[t, 1:2, :] = local_ref[t : t + 1, :]
    pltpu.make_async_copy(sum_scr, sum_scr, sem_out).wait()


def weigh(slot, fetched, ids1, ids2, ids3, rank, local, points, devices):
    n = points.shape[0]
    need = slot.shape[0]
    subs = local.shape[0]
    return pl.pallas_call(
        weigh_kernel,
        grid_spec=pltpu.PrefetchScalarGridSpec(
            num_scalar_prefetch=1,
            grid=(1,),
            in_specs=[
                ANY,
                full((n, 128)),
                full((1, n)),
                full((1, n)),
                full((1, n)),
                full((n, 128)),
                full((subs, CAP2)),
                full((n, D)),
            ],
            out_specs=[
                ANY,
                full((devices, BLK, TILE + 128)),
                full((subs, BLK, CAP2)),
            ],
            scratch_shapes=[
                pltpu.VMEM((need, BLK, D), BF),
                pltpu.VMEM((need, BLK, D), BF),
                pltpu.VMEM((n, 128), F32),
                pltpu.VMEM((devices, BLK, 128), F32),
                pltpu.SemaphoreType.DMA,
                pltpu.SemaphoreType.DMA,
            ],
        ),
        out_shape=[
            jax.ShapeDtypeStruct(fetched.shape, BF),
            jax.ShapeDtypeStruct((devices, BLK, TILE + 128), BF),
            jax.ShapeDtypeStruct((subs, BLK, CAP2), F32),
        ],
        name="weigh",
    )(
        slot,
        fetched,
        jnp.broadcast_to(ids1[:, None], (n, 128)),
        ids1.reshape(1, n),
        ids2.reshape(1, n),
        ids3.reshape(1, n),
        rank,
        local,
        points,
    )


def level3_kernel(place, small_ref, cent_ref, out_ref):
    total = jnp.sum(small_ref[...].astype(F32), axis=0)
    lane = iota((BLK, 128), 1)
    ext = total[:, TILE:]
    mass = jnp.sum(jnp.where((lane == 4) | (lane == 5), ext, 0.0), axis=1, keepdims=True)
    new = (cent_ref[...].astype(F32) + total[:, 0:TILE]) / (1.0 + mass)
    out_ref[...] = jnp.broadcast_to(new.astype(BF)[None], out_ref.shape)


def level3(me, small, centroids3):
    devices = small.shape[0]
    wide = D // TILE
    return pl.pallas_call(
        level3_kernel,
        grid_spec=pltpu.PrefetchScalarGridSpec(
            num_scalar_prefetch=1,
            grid=(1,),
            in_specs=[
                full(small.shape),
                pl.BlockSpec((BLK, TILE), lambda i, place: (place[0], place[1])),
            ],
            out_specs=full((devices, BLK, TILE)),
        ),
        out_shape=jax.ShapeDtypeStruct((devices, BLK, TILE), BF),
        name="level3",
    )(jnp.stack([me // wide, me % wide]).astype(I32), small, centroids3)


def level2_kernel(meta_ref, pts_ref, cent_ref, out_ref):
    step = pl.program_id(0)
    count = out_ref.shape[0]
    subs = meta_ref.shape[0]
    rows = (iota((count, CAP2), 0) + step * count).astype(F32)
    hot = jnp.concatenate(
        [
            jnp.where(
                jnp.broadcast_to(meta_ref[t, 1:2, :], (count, CAP2)) == rows,
                jnp.broadcast_to(meta_ref[t, 0:1, :], (count, CAP2)),
                0.0,
            )
            for t in range(subs)
        ],
        axis=1,
    )
    sums = jnp.dot(hot.astype(BF), pts_ref[...], preferred_element_type=F32)
    mass = jnp.sum(hot, axis=1, keepdims=True)
    out_ref[...] = (cent_ref[...].astype(F32) + sums) / (1.0 + mass)


def level2(meta, routed, centroids2):
    rows = centroids2.shape[0]
    count = 128
    return pl.pallas_call(
        level2_kernel,
        grid=(rows // count,),
        in_specs=[
            full(meta.shape),
            full(routed.shape),
            pl.BlockSpec((count, D), lambda i: (i, 0)),
        ],
        out_specs=pl.BlockSpec((count, D), lambda i: (i, 0)),
        out_shape=jax.ShapeDtypeStruct((rows, D), F32),
        name="level2",
    )(meta, routed, centroids2)


def level1_kernel(asked, back_ref, small_ref, cent_ref, out_ref, acc_scr, mass_scr, stage, sem):
    blocks = acc_scr.shape[0]
    slots = back_ref.shape[0]
    lane = iota((BLK, 128), 1)
    part = stage.shape[1]

    def begin(g, carry):
        at = pl.ds(pl.multiple_of(g * 8, 8), 8)
        acc_scr[at] = cent_ref[at].astype(F32)
        mass_scr[at] = jnp.zeros((8, BLK, 128), F32)
        return carry

    lax.fori_loop(0, blocks // 8, begin, 0)

    def add(s, carry):
        b = asked[s]

        @pl.when(b >= 0)
        def _():
            acc_scr[b] = acc_scr[b] + back_ref[s].astype(F32)
            at = (s % CAP) * 2
            m = small_ref[s // CAP, :, TILE:].astype(F32)
            mass_scr[b] = mass_scr[b] + jnp.where((lane == at) | (lane == at + 1), m, 0.0)

        return carry

    lax.fori_loop(0, slots, add, 0, unroll=4)

    for g in range(blocks // part):
        k = g % 2
        view = out_ref.at[pl.ds(g * part, part)]
        if g >= 2:
            pltpu.make_async_copy(stage.at[k], view, sem.at[k]).wait()
        total = jnp.sum(mass_scr[g * part : (g + 1) * part], axis=2, keepdims=True)
        stage[k] = acc_scr[g * part : (g + 1) * part] / (1.0 + total)
        pltpu.make_async_copy(stage.at[k], view, sem.at[k]).start()
    for k in range(2):
        pltpu.make_async_copy(stage.at[k], out_ref.at[pl.ds(0, part)], sem.at[k]).wait()


def level1(asked, back, small, table):
    blocks = table.shape[0]
    whole = pl.BlockSpec(memory_space=pltpu.VMEM)
    return pl.pallas_call(
        level1_kernel,
        grid_spec=pltpu.PrefetchScalarGridSpec(
            num_scalar_prefetch=1,
            grid=(),
            in_specs=[whole, whole, whole],
            out_specs=ANY,
            scratch_shapes=[
                pltpu.VMEM((blocks, BLK, D), F32),
                pltpu.VMEM((blocks, BLK, 128), F32),
                pltpu.VMEM((2, 32, BLK, D), F32),
                pltpu.SemaphoreType.DMA((2,)),
            ],
        ),
        out_shape=jax.ShapeDtypeStruct((blocks, BLK, D), F32),
        name="level1",
    )(asked, back, small, table)


def shards(points, level1_ids, level2_ids, level3_ids, needed, centroids1, centroids2, centroids3):
    both = ("grp", "sub")
    devices = lax.axis_size(both)
    subs = lax.axis_size("sub")
    me = lax.axis_index(both)
    blocks = K1_DEV // BLK
    wanted = needed[0]
    need = wanted.shape[0]

    def swap(values, axes):
        return lax.all_to_all(values, axes, split_axis=0, concat_axis=0, tiled=True)

    owners = wanted // blocks
    same = (owners[:, None] == owners[None, :]) & (
        jnp.arange(need)[None, :] < jnp.arange(need)[:, None]
    )
    slot = owners * CAP + jnp.sum(same.astype(I32), axis=1)
    requests = (
        jnp.sum(
            jnp.where(
                slot[:, None] == jnp.arange(devices * CAP)[None, :],
                wanted[:, None] % blocks + 1,
                0,
            ),
            axis=0,
        )
        - 1
    )
    asked = swap(requests.reshape(devices, 1, CAP), both).reshape(devices * CAP)
    routed, rank, local = route(level2_ids, points, subs)
    routed = swap(routed.reshape(subs, CAP2, D), "sub").reshape(subs * CAP2, D)
    table = centroids1.reshape(blocks, BLK, D)
    fetched = swap(serve(asked, table), both)
    sums, small, meta = weigh(
        slot, fetched, level1_ids, level2_ids, level3_ids, rank, local, points, devices
    )
    small = swap(small, both)
    back = swap(sums, both)
    meta = swap(meta, "sub")
    tiles = swap(level3(me, small, centroids3), both)
    level2_new = level2(meta, routed, centroids2[0])[None]
    level1_new = level1(asked, back, small, table).reshape(K1_DEV, D)
    wide = D // TILE
    level3_new = (
        tiles.reshape(K3 // BLK, wide, BLK, TILE).transpose(0, 2, 1, 3).reshape(K3, D).astype(F32)
    )
    return level1_new, level2_new, level3_new


def solution(mesh):
    placed = (
        P(("grp", "sub"), None),
        P(("grp", "sub")),
        P(("grp", "sub")),
        P(("grp", "sub")),
        P(("grp", "sub"), None),
        P(("grp", "sub"), None),
        P("grp", "sub", None),
        P(),
    )
    return jax.shard_map(
        shards,
        mesh=mesh,
        in_specs=placed,
        out_specs=(P(("grp", "sub"), None), P("grp", "sub", None), P()),
        check_vma=False,
    )
```

```python
import jax
import jax.numpy as jnp
from jax import lax
from jax.experimental import pallas as pl
from jax.experimental.pallas import tpu as pltpu
from jax.sharding import PartitionSpec as P


D = 1024
K1_DEV = 2048
BLK = 8
CAP = 2
K2 = 8192
K3 = 256
CAP2 = 128
TILE = 256
BF = jnp.bfloat16
F32 = jnp.float32
I32 = jnp.int32


def full(shape):
    return pl.BlockSpec(shape, lambda *_: (0,) * len(shape))


ANY = pl.BlockSpec(memory_space=pl.ANY)


def iota(shape, axis):
    return lax.broadcasted_iota(I32, shape, axis)


def route_kernel(place, ids_ref, pts_ref, *refs):
    pieces, (slot_ref, aux_ref, slot_scr) = refs[:-3], refs[-3:]
    n = pts_ref.shape[0]
    subs = len(pieces)
    rows = K2 // subs
    ids = ids_ref[...]
    owner = ids // rows
    local = ids - owner * rows
    hot = (jnp.broadcast_to(owner, (subs, n)) == iota((subs, n), 0)).astype(F32)
    upper = (iota((n, n), 0) < iota((n, n), 1)).astype(F32).astype(BF)
    before = jnp.dot(hot.astype(BF), upper, preferred_element_type=F32)
    rank = jnp.sum(before * hot, axis=0, keepdims=True).astype(I32)
    slot_ref[...] = owner * CAP2 + rank
    away = owner - place[0]
    away = jnp.where(away < 0, away + subs, away)
    slot_scr[...] = away * CAP2 + rank
    packed = (rank % 16) + 16 * local
    col = jnp.transpose(jnp.broadcast_to(packed.astype(F32), (128, n))).astype(I32)
    rank_col = col % 16
    local_col = col // 16
    lane = iota((n, 128), 1)
    aux = jnp.where(lane == rank_col + 8, 1, 0)
    aux = aux + jnp.where(lane == rank_col + 24, local_col % 256, 0)
    aux = aux + jnp.where(lane == rank_col + 40, local_col // 256, 0)
    aux_ref[...] = aux.astype(F32)
    group = 8
    chunk = group * CAP2
    for c in range(subs // group):
        slots = jnp.broadcast_to(slot_scr[...], (chunk, n))
        perm = (slots == iota((chunk, n), 0) + c * chunk).astype(F32).astype(BF)
        moved = jnp.dot(perm, pts_ref[...], preferred_element_type=F32).astype(BF)
        for k in range(group):
            pieces[c * group + k][...] = moved[k * CAP2 : (k + 1) * CAP2, :]


def route(place, ids2, points, subs):
    n = points.shape[0]
    out = pl.pallas_call(
        route_kernel,
        grid_spec=pltpu.PrefetchScalarGridSpec(
            num_scalar_prefetch=1,
            grid=(1,),
            in_specs=[full((1, n)), full((n, D))],
            out_specs=[full((CAP2, D))] * subs + [full((1, n)), full((n, 128))],
            scratch_shapes=[pltpu.VMEM((1, n), I32)],
        ),
        out_shape=[jax.ShapeDtypeStruct((CAP2, D), BF)] * subs
        + [jax.ShapeDtypeStruct((1, n), I32), jax.ShapeDtypeStruct((n, 128), F32)],
        name="route",
    )(place, ids2.reshape(1, n), points)
    return out[:subs], out[subs], out[subs + 1]


def serve_kernel(asked, table_ref, out_ref, sem):
    count = out_ref.shape[0]

    def one(i, carry):
        pltpu.make_async_copy(table_ref.at[jnp.maximum(asked[i], 0)], out_ref.at[i], sem).start()
        return carry

    lax.fori_loop(0, count, one, 0, unroll=8)
    pltpu.make_async_copy(out_ref, out_ref, sem).wait()


def serve(asked, table):
    return pl.pallas_call(
        serve_kernel,
        grid_spec=pltpu.PrefetchScalarGridSpec(
            num_scalar_prefetch=1,
            grid=(),
            in_specs=[pl.BlockSpec(memory_space=pltpu.VMEM)],
            out_specs=ANY,
            scratch_shapes=[pltpu.SemaphoreType.DMA],
        ),
        out_shape=jax.ShapeDtypeStruct((asked.shape[0], BLK, D), BF),
        name="serve",
    )(asked, table)


def weigh_kernel(
    slot, place, fetched_ref, col1_ref, row1_ref, row3_ref, slot2_ref, aux_ref, pts_ref, out_ref,
    near_scr, sum_scr, w_scr, ext_scr, small_scr, sem_in, sem_out,
):
    n = pts_ref.shape[0]
    need = near_scr.shape[0]
    devices = out_ref.shape[0]
    rows = need * BLK

    def fetch(e, carry):
        pltpu.make_async_copy(fetched_ref.at[slot[e]], near_scr.at[e], sem_in).start()
        return carry

    lax.fori_loop(0, need, fetch, 0, unroll=8)
    ext_scr[...] = jnp.zeros(ext_scr.shape, F32)
    pltpu.make_async_copy(near_scr, near_scr, sem_in).wait()
    near = near_scr[...].reshape(rows, D)
    step = 512
    for c in range(n // step):
        col = col1_ref[c * step : (c + 1) * step, :]
        hot = jnp.concatenate(
            [(col == iota((step, 128), 1) + 128 * t).astype(F32) for t in range(rows // 128)], axis=1
        ).astype(BF)
        nearest = jnp.dot(hot, near, preferred_element_type=F32)
        diff = pts_ref[c * step : (c + 1) * step, :].astype(F32) - nearest
        spread = jnp.sum(diff * diff, axis=1, keepdims=True) / D
        w = (1.0 / (1.0 + spread)).astype(BF).astype(F32)
        w_scr[c * step : (c + 1) * step, :] = jnp.broadcast_to(w, (step, 128))
    w_col = w_scr[...]
    w_row = jnp.transpose(w_col)[0:1, :]

    def weighted(row_ids, count, first):
        same = jnp.broadcast_to(row_ids, (count, n)) == iota((count, n), 0) + first
        return jnp.where(same, jnp.broadcast_to(w_row, (count, n)), 0.0)

    lane = iota((BLK, 128), 1)

    part = 512
    for c in range(rows // part):
        hot1 = weighted(row1_ref[...], part, c * part)
        sums1 = jnp.dot(hot1.astype(BF), pts_ref[...], preferred_element_type=F32).astype(BF)
        sum_scr[c * (part // BLK) : (c + 1) * (part // BLK)] = sums1.reshape(part // BLK, BLK, D)
        mass1 = jnp.broadcast_to(jnp.sum(hot1, axis=1, keepdims=True), (part, 128))
        for k in range(part // BLK):
            e = c * (part // BLK) + k
            s = slot[e]
            o = s // CAP
            at = s - o * CAP
            pltpu.make_async_copy(
                sum_scr.at[e], out_ref.at[o, :, pl.ds(pl.multiple_of(at * D, D), D)], sem_out
            ).start()
            m = mass1[k * BLK : (k + 1) * BLK, :]
            high = m.astype(BF).astype(F32)
            ext_scr[o] = ext_scr[o] + jnp.where(lane == 2 * at, high, 0.0) + jnp.where(
                lane == 2 * at + 1, m - high, 0.0
            )

    cells = slot2_ref[...] // 16
    count = K2 // 512 * CAP2 // 16
    hot_cell = (jnp.broadcast_to(cells, (count, n)) == iota((count, n), 0)).astype(F32).astype(BF)
    aux = aux_ref[...]
    aux = jnp.where(iota((n, 128), 1) < 24, aux * w_col, aux).astype(BF)
    table = jnp.dot(hot_cell, aux, preferred_element_type=F32)
    for t in range(count // BLK):
        o = place[1] + t
        ext_scr[o] = ext_scr[o] + table[t * BLK : (t + 1) * BLK, :]

    tile = iota((K3, 128), 1)
    hot3 = weighted(row3_ref[...], K3, 0)
    sums3 = jnp.dot(hot3.astype(BF), pts_ref[...], preferred_element_type=F32).astype(BF)
    mass3 = jnp.broadcast_to(jnp.sum(hot3, axis=1, keepdims=True), (K3, 128))
    high3 = mass3.astype(BF).astype(F32)
    ext3 = jnp.where(tile == 4, high3, 0.0) + jnp.where(tile == 5, mass3 - high3, 0.0)
    wide = D // TILE
    for o in range(devices):
        b, c = o // wide, o % wide
        small_scr[o, :, 0:TILE] = sums3[BLK * b : BLK * (b + 1), TILE * c : TILE * (c + 1)]
        small_scr[o, :, TILE:] = (ext_scr[o] + ext3[BLK * b : BLK * (b + 1), :]).astype(BF)
    tail = pltpu.make_async_copy(small_scr, out_ref.at[:, :, pl.ds(CAP * D, TILE + 128)], sem_in)
    tail.start()
    pltpu.make_async_copy(sum_scr, sum_scr, sem_out).wait()
    tail.wait()


def weigh(slot, place, fetched, ids1, ids3, slot2, aux, points, devices):
    n = points.shape[0]
    need = slot.shape[0]
    return pl.pallas_call(
        weigh_kernel,
        grid_spec=pltpu.PrefetchScalarGridSpec(
            num_scalar_prefetch=2,
            grid=(1,),
            in_specs=[
                ANY,
                full((n, 128)),
                full((1, n)),
                full((1, n)),
                full((1, n)),
                full((n, 128)),
                full((n, D)),
            ],
            out_specs=ANY,
            scratch_shapes=[
                pltpu.VMEM((need, BLK, D), BF),
                pltpu.VMEM((need, BLK, D), BF),
                pltpu.VMEM((n, 128), F32),
                pltpu.VMEM((devices, BLK, 128), F32),
                pltpu.VMEM((devices, BLK, TILE + 128), BF),
                pltpu.SemaphoreType.DMA,
                pltpu.SemaphoreType.DMA,
            ],
        ),
        out_shape=jax.ShapeDtypeStruct((devices, BLK, CAP * D + TILE + 128), BF),
        name="weigh",
    )(
        slot,
        place,
        fetched,
        jnp.broadcast_to(ids1[:, None], (n, 128)),
        ids1.reshape(1, n),
        ids3.reshape(1, n),
        slot2,
        aux,
        points,
    )


def level3_kernel(place, tile_ref, ext_ref, cent_ref, out_ref):
    total = jnp.sum(tile_ref[...].astype(F32), axis=0)
    ext = jnp.sum(ext_ref[...].astype(F32), axis=0)
    lane = iota((BLK, 128), 1)
    mass = jnp.sum(jnp.where((lane == 4) | (lane == 5), ext, 0.0), axis=1, keepdims=True)
    new = (cent_ref[...].astype(F32) + total) / (1.0 + mass)
    out_ref[...] = jnp.broadcast_to(new.astype(BF)[None], out_ref.shape)


def level3(place, back, centroids3):
    devices = back.shape[0]
    return pl.pallas_call(
        level3_kernel,
        grid_spec=pltpu.PrefetchScalarGridSpec(
            num_scalar_prefetch=1,
            grid=(1,),
            in_specs=[
                pl.BlockSpec((devices, BLK, TILE), lambda i, place: (0, 0, CAP * D // TILE)),
                pl.BlockSpec((devices, BLK, 128), lambda i, place: (0, 0, (CAP * D + TILE) // 128)),
                pl.BlockSpec((BLK, TILE), lambda i, place: (place[2], place[3])),
            ],
            out_specs=full((devices, BLK, TILE)),
        ),
        out_shape=jax.ShapeDtypeStruct((devices, BLK, TILE), BF),
        name="level3",
    )(place, back, back, centroids3)


def level2_kernel(place, ext_ref, cent_ref, *refs):
    pieces, (out_ref, pts_scr, hot_scr, w_scr, id_scr, mass_scr, sem) = refs[:-7], refs[-7:]
    rows, width = out_ref.shape
    step = pl.program_id(0)
    subs = len(pieces)

    @pl.when(step == 0)
    def _():
        for k in range(subs):
            source = place[0] - k
            source = jnp.where(source < 0, source + subs, source)
            at = pl.ds(pl.multiple_of(source * CAP2, CAP2), CAP2)
            pltpu.make_async_copy(pieces[k], pts_scr.at[at], sem).start()
        cells = ext_ref[...].astype(F32).reshape(subs * BLK, 128).astype(BF)
        lane_in = iota((128, 128), 0)
        lane_out = iota((128, 128), 1)
        own = iota((subs * BLK, 128), 1) // 16 == iota((subs * BLK, 128), 0) % BLK

        def unpack(first):
            spread = (lane_in == first + lane_out % 16).astype(F32).astype(BF)
            wide = jnp.dot(cells, spread, preferred_element_type=F32)
            return jnp.sum(jnp.where(own, wide, 0.0).reshape(subs, BLK, 128), axis=1)

        w_scr[...] = unpack(8)
        id_scr[...] = unpack(24) + 256.0 * unpack(40)
        ids = iota((rows, CAP2), 0).astype(F32)
        mass = jnp.zeros((rows, CAP2), F32)
        for t in range(subs):
            hot = jnp.where(
                jnp.broadcast_to(id_scr[t : t + 1, :], (rows, CAP2)) == ids,
                jnp.broadcast_to(w_scr[t : t + 1, :], (rows, CAP2)),
                0.0,
            )
            mass = mass + hot
            hot_scr[:, t * CAP2 : (t + 1) * CAP2] = hot.astype(BF)
        total = jnp.sum(mass, axis=1, keepdims=True)
        mass_scr[...] = jnp.broadcast_to(1.0 + total, (rows, 128))
        pltpu.make_async_copy(pts_scr, pts_scr, sem).wait()

    at = pl.ds(pl.multiple_of(step * width, width), width)
    sums = jnp.dot(hot_scr[...], pts_scr[:, at], preferred_element_type=F32)
    out_ref[...] = (cent_ref[...].astype(F32) + sums) / mass_scr[:, 0:1]


def level2(place, back, pieces, centroids2):
    rows = centroids2.shape[0]
    subs = len(pieces)
    width = 256
    return pl.pallas_call(
        level2_kernel,
        grid_spec=pltpu.PrefetchScalarGridSpec(
            num_scalar_prefetch=1,
            grid=(D // width,),
            in_specs=[
                pl.BlockSpec(
                    (subs, BLK, 128), lambda i, place: (place[4], 0, (CAP * D + TILE) // 128)
                ),
                pl.BlockSpec((rows, width), lambda i, place: (0, i)),
            ]
            + [ANY] * subs,
            out_specs=pl.BlockSpec((rows, width), lambda i, place: (0, i)),
            scratch_shapes=[
                pltpu.VMEM((subs * CAP2, D), BF),
                pltpu.VMEM((rows, subs * CAP2), BF),
                pltpu.VMEM((subs, CAP2), F32),
                pltpu.VMEM((subs, CAP2), F32),
                pltpu.VMEM((rows, 128), F32),
                pltpu.SemaphoreType.DMA,
            ],
        ),
        out_shape=jax.ShapeDtypeStruct((rows, D), F32),
        name="level2",
    )(place, back, centroids2, *pieces)


def level1_kernel(
    asked, order, start, back_ref, cent_ref, out_ref,
    back_scr, cent_scr, mass_scr, stage, sem_back, sem_cent, sem_out,
):
    parts = cent_scr.shape[0]
    part = cent_scr.shape[1]
    lane = iota((BLK, 128), 1)
    back = pltpu.make_async_copy(back_ref, back_scr, sem_back)
    back.start()

    def cents(g):
        return pltpu.make_async_copy(
            cent_ref.at[pl.ds(g * part, part)], cent_scr.at[g], sem_cent.at[g]
        )

    def out(g):
        return pltpu.make_async_copy(
            stage.at[g % 2], out_ref.at[pl.ds(g * part, part)], sem_out.at[g % 2]
        )

    for g in range(parts):
        cents(g).start()
    for g in range(parts):
        k = g % 2
        if g >= 2:
            out(g - 2).wait()
        cents(g).wait()
        stage[k] = cent_scr[g].astype(F32)
        mass_scr[...] = jnp.zeros(mass_scr.shape, F32)
        if g == 0:
            back.wait()

        def add(i, carry):
            s = order[i]
            b = asked[s] - g * part
            o = s // CAP
            at = s - o * CAP
            sums = back_scr[o, :, pl.ds(pl.multiple_of(at * D, D), D)]
            stage[k, b] = stage[k, b] + sums.astype(F32)
            m = back_scr[o, :, CAP * D + TILE :].astype(F32)
            mass_scr[b] = mass_scr[b] + jnp.where(
                (lane == 2 * at) | (lane == 2 * at + 1), m, 0.0
            )
            return carry

        lax.fori_loop(start[g], start[g + 1], add, 0)
        total = jnp.sum(mass_scr[...], axis=2, keepdims=True)
        stage[k] = stage[k] * (1.0 / (1.0 + total))
        out(g).start()
    for g in range(parts - 2, parts):
        out(g).wait()


def level1(asked, order, start, back, table):
    blocks = table.shape[0]
    parts = start.shape[0] - 1
    part = blocks // parts
    return pl.pallas_call(
        level1_kernel,
        grid_spec=pltpu.PrefetchScalarGridSpec(
            num_scalar_prefetch=3,
            grid=(),
            in_specs=[ANY, ANY],
            out_specs=ANY,
            scratch_shapes=[
                pltpu.VMEM(back.shape, BF),
                pltpu.VMEM((parts, part, BLK, D), BF),
                pltpu.VMEM((part, BLK, 128), F32),
                pltpu.VMEM((2, part, BLK, D), F32),
                pltpu.SemaphoreType.DMA,
                pltpu.SemaphoreType.DMA((parts,)),
                pltpu.SemaphoreType.DMA((2,)),
            ],
        ),
        out_shape=jax.ShapeDtypeStruct((blocks, BLK, D), F32),
        name="level1",
    )(asked, order, start, back, table)


def shards(points, level1_ids, level2_ids, level3_ids, needed, centroids1, centroids2, centroids3):
    both = ("grp", "sub")
    devices = lax.axis_size(both)
    subs = lax.axis_size("sub")
    group = lax.axis_index("grp")
    sub = lax.axis_index("sub")
    me = group * subs + sub
    blocks = K1_DEV // BLK
    wide = D // TILE
    wanted = needed[0]
    need = wanted.shape[0]
    place = jnp.stack([sub, group * subs, me >> 2, me & 3, group]).astype(I32)

    def swap(values, axes):
        return lax.all_to_all(values, axes, split_axis=0, concat_axis=0, tiled=True)

    owners = wanted // blocks
    same = (owners[:, None] == owners[None, :]) & (
        jnp.arange(need)[None, :] < jnp.arange(need)[:, None]
    )
    slot = owners * CAP + jnp.sum(same.astype(I32), axis=1)
    requests = (
        jnp.sum(
            jnp.where(
                slot[:, None] == jnp.arange(devices * CAP)[None, :],
                wanted[:, None] % blocks + 1,
                0,
            ),
            axis=0,
        )
        - 1
    )
    asked = swap(requests.reshape(devices, 1, CAP), both).reshape(devices * CAP)
    pieces, slot2, aux = route(place, level2_ids, points, subs)
    asked, aux = lax.optimization_barrier((asked, aux))
    pieces = list(pieces)
    for k in range(1, subs):
        pieces[k] = lax.ppermute(pieces[k], "sub", [(i, (i + k) % subs) for i in range(subs)])
    table = centroids1.reshape(blocks, BLK, D)
    served = serve(asked, table)
    fetched = swap(served, both)
    count = devices * CAP
    key = jnp.where(asked < 0, blocks, asked) * count + jnp.arange(count)
    position = jnp.sum((key[None, :] < key[:, None]).astype(I32), axis=1)
    order = jnp.sum(
        jnp.where(position[:, None] == jnp.arange(count)[None, :], jnp.arange(count)[:, None], 0),
        axis=0,
    )
    parts = 8
    bounds = jnp.arange(parts + 1) * (blocks // parts) * count
    start = jnp.sum((key[None, :] < bounds[:, None]).astype(I32), axis=1)
    slot, order, start = lax.optimization_barrier((slot, order, start))
    sums = weigh(slot, place, fetched, level1_ids, level3_ids, slot2, aux, points, devices)
    back = swap(sums, both)
    tiles = level3(place, back, centroids3)
    tiles = swap(tiles, both)
    level2_new = level2(place, back, pieces, centroids2[0])[None]
    level1_new = level1(asked, order, start, back, table).reshape(K1_DEV, D)
    level3_new = (
        tiles.reshape(K3 // BLK, wide, BLK, TILE).transpose(0, 2, 1, 3).reshape(K3, D).astype(F32)
    )
    return level1_new, level2_new, level3_new


def solution(mesh):
    placed = (
        P(("grp", "sub"), None),
        P(("grp", "sub")),
        P(("grp", "sub")),
        P(("grp", "sub")),
        P(("grp", "sub"), None),
        P(("grp", "sub"), None),
        P("grp", "sub", None),
        P(),
    )

    return jax.shard_map(
        shards,
        mesh=mesh,
        in_specs=placed,
        out_specs=(P(("grp", "sub"), None), P("grp", "sub", None), P()),
        check_vma=False,
    )
```

```python
import jax
import jax.numpy as jnp
from jax import lax
from jax.experimental import pallas as pl
from jax.experimental.pallas import tpu as pltpu
from jax.sharding import PartitionSpec as P


D = 1024
K1_DEV = 2048
BLK = 8
CAP = 2
K2 = 8192
K3 = 256
CAP2 = 128
TILE = 256
BF = jnp.bfloat16
F32 = jnp.float32
I32 = jnp.int32


def full(shape):
    return pl.BlockSpec(shape, lambda *_: (0,) * len(shape))


ANY = pl.BlockSpec(memory_space=pl.ANY)


def iota(shape, axis):
    return lax.broadcasted_iota(I32, shape, axis)


def route_kernel(place, ids_ref, pts_ref, *refs):
    pieces, (slot_ref, aux_ref, slot_scr) = refs[:-3], refs[-3:]
    n = pts_ref.shape[0]
    subs = len(pieces)
    rows = K2 // subs
    ids = ids_ref[...]
    owner = ids // rows
    local = ids - owner * rows
    hot = (jnp.broadcast_to(owner, (subs, n)) == iota((subs, n), 0)).astype(F32)
    upper = (iota((n, n), 0) < iota((n, n), 1)).astype(F32).astype(BF)
    before = jnp.dot(hot.astype(BF), upper, preferred_element_type=F32)
    rank = jnp.sum(before * hot, axis=0, keepdims=True).astype(I32)
    slot_ref[...] = owner * CAP2 + rank
    away = owner - place[0]
    away = jnp.where(away < 0, away + subs, away)
    slot_scr[...] = away * CAP2 + rank
    packed = (rank % 16) + 16 * local
    col = jnp.transpose(jnp.broadcast_to(packed.astype(F32), (128, n))).astype(I32)
    rank_col = col % 16
    local_col = col // 16
    lane = iota((n, 128), 1)
    aux = jnp.where(lane == rank_col + 8, 1, 0)
    aux = aux + jnp.where(lane == rank_col + 24, local_col % 256, 0)
    aux = aux + jnp.where(lane == rank_col + 40, local_col // 256, 0)
    aux_ref[...] = aux.astype(F32)
    group = 8
    chunk = group * CAP2
    for c in range(subs // group):
        slots = jnp.broadcast_to(slot_scr[...], (chunk, n))
        perm = (slots == iota((chunk, n), 0) + c * chunk).astype(F32).astype(BF)
        moved = jnp.dot(perm, pts_ref[...], preferred_element_type=F32).astype(BF)
        for k in range(group):
            pieces[c * group + k][...] = moved[k * CAP2 : (k + 1) * CAP2, :]


def route(place, ids2, points, subs):
    n = points.shape[0]
    out = pl.pallas_call(
        route_kernel,
        grid_spec=pltpu.PrefetchScalarGridSpec(
            num_scalar_prefetch=1,
            grid=(1,),
            in_specs=[full((1, n)), full((n, D))],
            out_specs=[full((CAP2, D))] * subs + [full((1, n)), full((n, 128))],
            scratch_shapes=[pltpu.VMEM((1, n), I32)],
        ),
        out_shape=[jax.ShapeDtypeStruct((CAP2, D), BF)] * subs
        + [jax.ShapeDtypeStruct((1, n), I32), jax.ShapeDtypeStruct((n, 128), F32)],
        name="route",
    )(place, ids2.reshape(1, n), points)
    return out[:subs], out[subs], out[subs + 1]


def serve_kernel(asked, table_ref, out_ref, sem):
    count = out_ref.shape[0]

    def one(i, carry):
        for k in range(CAP):
            block = jnp.maximum(asked[i, k], 0)
            pltpu.make_async_copy(table_ref.at[block], out_ref.at[CAP * i + k], sem).start()
        return carry

    lax.fori_loop(0, count // CAP, one, 0, unroll=8)
    pltpu.make_async_copy(out_ref, out_ref, sem).wait()


def serve(asked, table):
    return pl.pallas_call(
        serve_kernel,
        grid_spec=pltpu.PrefetchScalarGridSpec(
            num_scalar_prefetch=1,
            grid=(),
            in_specs=[pl.BlockSpec(memory_space=pltpu.VMEM)],
            out_specs=ANY,
            scratch_shapes=[pltpu.SemaphoreType.DMA],
        ),
        out_shape=jax.ShapeDtypeStruct((asked.shape[0] * CAP, BLK, D), BF),
        name="serve",
    )(asked, table)


def weigh_kernel(
    slot, place, fetched_ref, col1_ref, row1_ref, row3_ref, slot2_ref, aux_ref, pts_ref, out_ref,
    near_scr, sum_scr, w_scr, ext_scr, small_scr, sem_in, sem_out,
):
    n = pts_ref.shape[0]
    need = near_scr.shape[0]
    devices = out_ref.shape[0]
    rows = need * BLK

    def fetch(e, carry):
        pltpu.make_async_copy(fetched_ref.at[slot[e]], near_scr.at[e], sem_in).start()
        return carry

    lax.fori_loop(0, need, fetch, 0, unroll=8)
    ext_scr[...] = jnp.zeros(ext_scr.shape, F32)
    pltpu.make_async_copy(near_scr, near_scr, sem_in).wait()
    near = near_scr[...].reshape(rows, D)
    step = 512
    for c in range(n // step):
        col = col1_ref[c * step : (c + 1) * step, :]
        hot = jnp.concatenate(
            [(col == iota((step, 128), 1) + 128 * t).astype(F32) for t in range(rows // 128)], axis=1
        ).astype(BF)
        nearest = jnp.dot(hot, near, preferred_element_type=F32)
        diff = pts_ref[c * step : (c + 1) * step, :].astype(F32) - nearest
        spread = jnp.sum(diff * diff, axis=1, keepdims=True) / D
        w = (1.0 / (1.0 + spread)).astype(BF).astype(F32)
        w_scr[c * step : (c + 1) * step, :] = jnp.broadcast_to(w, (step, 128))
    w_col = w_scr[...]
    w_row = jnp.transpose(w_col)[0:1, :]

    def weighted(row_ids, count, first):
        same = jnp.broadcast_to(row_ids, (count, n)) == iota((count, n), 0) + first
        return jnp.where(same, jnp.broadcast_to(w_row, (count, n)), 0.0)

    lane = iota((BLK, 128), 1)

    part = 512
    for c in range(rows // part):
        hot1 = weighted(row1_ref[...], part, c * part)
        sums1 = jnp.dot(hot1.astype(BF), pts_ref[...], preferred_element_type=F32).astype(BF)
        sum_scr[c * (part // BLK) : (c + 1) * (part // BLK)] = sums1.reshape(part // BLK, BLK, D)
        mass1 = jnp.broadcast_to(jnp.sum(hot1, axis=1, keepdims=True), (part, 128))
        for k in range(part // BLK):
            e = c * (part // BLK) + k
            s = slot[e]
            o = s // CAP
            at = s - o * CAP
            pltpu.make_async_copy(
                sum_scr.at[e], out_ref.at[o, :, pl.ds(pl.multiple_of(at * D, D), D)], sem_out
            ).start()
            m = mass1[k * BLK : (k + 1) * BLK, :]
            high = m.astype(BF).astype(F32)
            ext_scr[o] = ext_scr[o] + jnp.where(lane == 2 * at, high, 0.0) + jnp.where(
                lane == 2 * at + 1, m - high, 0.0
            )

    cells = slot2_ref[...] // 16
    count = K2 // 512 * CAP2 // 16
    hot_cell = (jnp.broadcast_to(cells, (count, n)) == iota((count, n), 0)).astype(F32).astype(BF)
    aux = aux_ref[...]
    aux = jnp.where(iota((n, 128), 1) < 24, aux * w_col, aux).astype(BF)
    table = jnp.dot(hot_cell, aux, preferred_element_type=F32)
    for t in range(count // BLK):
        o = place[1] + t
        ext_scr[o] = ext_scr[o] + table[t * BLK : (t + 1) * BLK, :]

    tile = iota((K3, 128), 1)
    hot3 = weighted(row3_ref[...], K3, 0)
    sums3 = jnp.dot(hot3.astype(BF), pts_ref[...], preferred_element_type=F32).astype(BF)
    mass3 = jnp.broadcast_to(jnp.sum(hot3, axis=1, keepdims=True), (K3, 128))
    high3 = mass3.astype(BF).astype(F32)
    ext3 = jnp.where(tile == 4, high3, 0.0) + jnp.where(tile == 5, mass3 - high3, 0.0)
    wide = D // TILE
    for o in range(devices):
        b, c = o // wide, o % wide
        small_scr[o, :, 0:TILE] = sums3[BLK * b : BLK * (b + 1), TILE * c : TILE * (c + 1)]
        small_scr[o, :, TILE:] = (ext_scr[o] + ext3[BLK * b : BLK * (b + 1), :]).astype(BF)
    tail = pltpu.make_async_copy(small_scr, out_ref.at[:, :, pl.ds(CAP * D, TILE + 128)], sem_in)
    tail.start()
    pltpu.make_async_copy(sum_scr, sum_scr, sem_out).wait()
    tail.wait()


def weigh(slot, place, fetched, ids1, ids3, slot2, aux, points, devices):
    n = points.shape[0]
    need = slot.shape[0]
    return pl.pallas_call(
        weigh_kernel,
        grid_spec=pltpu.PrefetchScalarGridSpec(
            num_scalar_prefetch=2,
            grid=(1,),
            in_specs=[
                ANY,
                full((n, 128)),
                full((1, n)),
                full((1, n)),
                full((1, n)),
                full((n, 128)),
                full((n, D)),
            ],
            out_specs=ANY,
            scratch_shapes=[
                pltpu.VMEM((need, BLK, D), BF),
                pltpu.VMEM((need, BLK, D), BF),
                pltpu.VMEM((n, 128), F32),
                pltpu.VMEM((devices, BLK, 128), F32),
                pltpu.VMEM((devices, BLK, TILE + 128), BF),
                pltpu.SemaphoreType.DMA,
                pltpu.SemaphoreType.DMA,
            ],
        ),
        out_shape=jax.ShapeDtypeStruct((devices, BLK, CAP * D + TILE + 128), BF),
        name="weigh",
    )(
        slot,
        place,
        fetched,
        jnp.broadcast_to(ids1[:, None], (n, 128)),
        ids1.reshape(1, n),
        ids3.reshape(1, n),
        slot2,
        aux,
        points,
    )


def level3_kernel(place, tile_ref, ext_ref, cent_ref, out_ref, own_ref):
    subs = own_ref.shape[0]
    own_ref[...] = ext_ref[pl.ds(pl.multiple_of(place[1], subs), subs)]
    total = jnp.sum(tile_ref[...].astype(F32), axis=0)
    ext = jnp.sum(ext_ref[...].astype(F32), axis=0)
    lane = iota((BLK, 128), 1)
    mass = jnp.sum(jnp.where((lane == 4) | (lane == 5), ext, 0.0), axis=1, keepdims=True)
    new = (cent_ref[...].astype(F32) + total) / (1.0 + mass)
    out_ref[...] = jnp.broadcast_to(new.astype(BF)[None], out_ref.shape)


def level3(place, back, centroids3, subs):
    devices = back.shape[0]
    return pl.pallas_call(
        level3_kernel,
        grid_spec=pltpu.PrefetchScalarGridSpec(
            num_scalar_prefetch=1,
            grid=(1,),
            in_specs=[
                pl.BlockSpec((devices, BLK, TILE), lambda i, place: (0, 0, CAP * D // TILE)),
                pl.BlockSpec((devices, BLK, 128), lambda i, place: (0, 0, (CAP * D + TILE) // 128)),
                pl.BlockSpec((BLK, TILE), lambda i, place: (place[2], place[3])),
            ],
            out_specs=[full((devices, BLK, TILE)), full((subs, BLK, 128))],
        ),
        out_shape=[
            jax.ShapeDtypeStruct((devices, BLK, TILE), BF),
            jax.ShapeDtypeStruct((subs, BLK, 128), BF),
        ],
        name="level3",
    )(place, back, back, centroids3)


def level2_kernel(place, ext_ref, cent_ref, *refs):
    pieces, (out_ref, pts_scr, hot_scr, w_scr, id_scr, mass_scr, sem) = refs[:-7], refs[-7:]
    rows, width = out_ref.shape
    step = pl.program_id(0)
    subs = len(pieces)

    @pl.when(step == 0)
    def _():
        for k in range(subs):
            source = place[0] - k
            source = jnp.where(source < 0, source + subs, source)
            at = pl.ds(pl.multiple_of(source * CAP2, CAP2), CAP2)
            pltpu.make_async_copy(pieces[k], pts_scr.at[at], sem).start()
        cells = ext_ref[...].astype(F32).reshape(subs * BLK, 128).astype(BF)
        lane_in = iota((128, 128), 0)
        lane_out = iota((128, 128), 1)
        own = iota((subs * BLK, 128), 1) // 16 == iota((subs * BLK, 128), 0) % BLK

        def unpack(first):
            spread = (lane_in == first + lane_out % 16).astype(F32).astype(BF)
            wide = jnp.dot(cells, spread, preferred_element_type=F32)
            return jnp.sum(jnp.where(own, wide, 0.0).reshape(subs, BLK, 128), axis=1)

        w_scr[...] = unpack(8)
        id_scr[...] = unpack(24) + 256.0 * unpack(40)
        ids = iota((rows, CAP2), 0).astype(F32)
        mass = jnp.zeros((rows, CAP2), F32)
        for t in range(subs):
            hot = jnp.where(
                jnp.broadcast_to(id_scr[t : t + 1, :], (rows, CAP2)) == ids,
                jnp.broadcast_to(w_scr[t : t + 1, :], (rows, CAP2)),
                0.0,
            )
            mass = mass + hot
            hot_scr[:, t * CAP2 : (t + 1) * CAP2] = hot.astype(BF)
        total = jnp.sum(mass, axis=1, keepdims=True)
        mass_scr[...] = jnp.broadcast_to(1.0 + total, (rows, 128))
        pltpu.make_async_copy(pts_scr, pts_scr, sem).wait()

    at = pl.ds(pl.multiple_of(step * width, width), width)
    sums = jnp.dot(hot_scr[...], pts_scr[:, at], preferred_element_type=F32)
    out_ref[...] = (cent_ref[...].astype(F32) + sums) / mass_scr[:, 0:1]


def level2(place, ext, pieces, centroids2):
    rows = centroids2.shape[0]
    subs = len(pieces)
    width = 256
    return pl.pallas_call(
        level2_kernel,
        grid_spec=pltpu.PrefetchScalarGridSpec(
            num_scalar_prefetch=1,
            grid=(D // width,),
            in_specs=[
                full(ext.shape),
                pl.BlockSpec((rows, width), lambda i, place: (0, i)),
            ]
            + [ANY] * subs,
            out_specs=pl.BlockSpec((rows, width), lambda i, place: (0, i)),
            scratch_shapes=[
                pltpu.VMEM((subs * CAP2, D), BF),
                pltpu.VMEM((rows, subs * CAP2), BF),
                pltpu.VMEM((subs, CAP2), F32),
                pltpu.VMEM((subs, CAP2), F32),
                pltpu.VMEM((rows, 128), F32),
                pltpu.SemaphoreType.DMA,
            ],
        ),
        out_shape=jax.ShapeDtypeStruct((rows, D), F32),
        compiler_params=pltpu.CompilerParams(vmem_limit_bytes=24 << 20),
        name="level2",
    )(place, ext, centroids2, *pieces)


def level1_kernel(
    order, start, back_ref, cent_ref, out_ref,
    back_scr, cent_scr, mass_scr, stage, sem_back, sem_cent, sem_out,
):
    parts = cent_scr.shape[0]
    part = cent_scr.shape[1]
    slots = CAP * back_scr.shape[0]
    lane = iota((BLK, 128), 1)
    back = pltpu.make_async_copy(back_ref, back_scr, sem_back)
    back.start()

    def cents(g):
        return pltpu.make_async_copy(
            cent_ref.at[pl.ds(g * part, part)], cent_scr.at[g], sem_cent.at[g]
        )

    def out(g):
        return pltpu.make_async_copy(
            stage.at[g % 2], out_ref.at[pl.ds(g * part, part)], sem_out.at[g % 2]
        )

    for g in range(parts):
        cents(g).start()
    for g in range(parts):
        k = g % 2
        if g >= 2:
            out(g - 2).wait()
        cents(g).wait()
        stage[k] = cent_scr[g].astype(F32)
        mass_scr[...] = jnp.zeros(mass_scr.shape, F32)
        if g == 0:
            back.wait()

        first, last = start[g], start[g + 1]

        def add(i, carry):
            loaded = []
            for j in range(4):
                at = first + 4 * i + j
                valid = at < last
                code = order[jnp.minimum(at, last - 1)]
                s = code % slots
                o = s // CAP
                side = s - o * CAP
                sums = back_scr[o, :, pl.ds(pl.multiple_of(side * D, D), D)].astype(F32)
                m = back_scr[o, :, CAP * D + TILE :].astype(F32)
                mine = (lane == 2 * side) | (lane == 2 * side + 1)
                loaded.append(
                    (
                        code // slots - g * part,
                        jnp.where(valid, sums, 0.0),
                        jnp.where(mine & valid, m, 0.0),
                    )
                )
            for b, sums, m in loaded:
                stage[k, b] = stage[k, b] + sums
                mass_scr[b] = mass_scr[b] + m
            return carry

        lax.fori_loop(0, (last - first + 3) // 4, add, 0)
        total = jnp.sum(mass_scr[...], axis=2, keepdims=True)
        stage[k] = stage[k] * (1.0 / (1.0 + total))
        out(g).start()
    for g in range(parts - 2, parts):
        out(g).wait()


def level1(order, start, back, table):
    blocks = table.shape[0]
    parts = start.shape[0] - 1
    part = blocks // parts
    return pl.pallas_call(
        level1_kernel,
        grid_spec=pltpu.PrefetchScalarGridSpec(
            num_scalar_prefetch=2,
            grid=(),
            in_specs=[ANY, ANY],
            out_specs=ANY,
            scratch_shapes=[
                pltpu.VMEM(back.shape, BF),
                pltpu.VMEM((parts, part, BLK, D), BF),
                pltpu.VMEM((part, BLK, 128), F32),
                pltpu.VMEM((2, part, BLK, D), F32),
                pltpu.SemaphoreType.DMA,
                pltpu.SemaphoreType.DMA((parts,)),
                pltpu.SemaphoreType.DMA((2,)),
            ],
        ),
        out_shape=jax.ShapeDtypeStruct((blocks, BLK, D), F32),
        name="level1",
    )(order, start, back, table)


def shards(points, level1_ids, level2_ids, level3_ids, needed, centroids1, centroids2, centroids3):
    both = ("grp", "sub")
    devices = lax.axis_size(both)
    subs = lax.axis_size("sub")
    group = lax.axis_index("grp")
    sub = lax.axis_index("sub")
    me = group * subs + sub
    blocks = K1_DEV // BLK
    wide = D // TILE
    wanted = needed[0]
    need = wanted.shape[0]
    place = jnp.stack([sub, group * subs, me >> 2, me & 3, group]).astype(I32)

    def swap(values, axes):
        return lax.all_to_all(values, axes, split_axis=0, concat_axis=0, tiled=True)

    owners = wanted // blocks
    same = (owners[:, None] == owners[None, :]) & (
        jnp.arange(need)[None, :] < jnp.arange(need)[:, None]
    )
    slot = owners * CAP + jnp.sum(same.astype(I32), axis=1)
    requests = (
        jnp.sum(
            jnp.where(
                slot[:, None] == jnp.arange(devices * CAP)[None, :],
                wanted[:, None] % blocks + 1,
                0,
            ),
            axis=0,
        )
        - 1
    )
    requests = jnp.pad(requests.reshape(devices, 1, CAP), ((0, 0), (0, 0), (0, 128 - CAP)))
    asked = swap(requests, both).reshape(devices, 128)
    pieces, slot2, aux = route(place, level2_ids, points, subs)
    asked, aux = lax.optimization_barrier((asked, aux))
    pieces = list(pieces)
    for k in range(1, subs):
        pieces[k] = lax.ppermute(pieces[k], "sub", [(i, (i + k) % subs) for i in range(subs)])
    table = centroids1.reshape(blocks, BLK, D)
    served = serve(asked, table)
    fetched = swap(served, both)
    count = devices * CAP
    flat = asked[:, :CAP].reshape(count)
    key = jnp.where(flat < 0, blocks, flat) * count + jnp.arange(count)
    position = jnp.sum((key[None, :] < key[:, None]).astype(I32), axis=1)
    order = jnp.sum(
        jnp.where(position[:, None] == jnp.arange(count)[None, :], key[:, None], 0), axis=0
    )
    parts = 8
    bounds = jnp.arange(parts + 1) * (blocks // parts) * count
    start = jnp.sum((key[None, :] < bounds[:, None]).astype(I32), axis=1)
    slot, order, start = lax.optimization_barrier((slot, order, start))
    sums = weigh(slot, place, fetched, level1_ids, level3_ids, slot2, aux, points, devices)
    back = swap(sums, both)
    tiles, ext = level3(place, back, centroids3, subs)
    tiles = swap(tiles, both)
    level2_new = level2(place, ext, pieces, centroids2[0])[None]
    level1_new = level1(order, start, back, table).reshape(K1_DEV, D)
    level3_new = (
        tiles.reshape(K3 // BLK, wide, BLK, TILE).transpose(0, 2, 1, 3).reshape(K3, D).astype(F32)
    )
    return level1_new, level2_new, level3_new


def solution(mesh):
    placed = (
        P(("grp", "sub"), None),
        P(("grp", "sub")),
        P(("grp", "sub")),
        P(("grp", "sub")),
        P(("grp", "sub"), None),
        P(("grp", "sub"), None),
        P("grp", "sub", None),
        P(),
    )

    return jax.shard_map(
        shards,
        mesh=mesh,
        in_specs=placed,
        out_specs=(P(("grp", "sub"), None), P("grp", "sub", None), P()),
        check_vma=False,
    )
```
